128 devices in a mesh: row: 8 (over y, core), col: 16 (over x, z).
Axes of the slice: x: 4, y: 4, z: 4, core: 2. Of those that a mesh axis runs over, the one named last changes fastest.
Arguments:
- valence_bands: bfloat16 [256, 96, 9216], P(('row', 'col')), may hold values from -6 to 6
- conduction_bands: bfloat16 [256, 96, 9216], P(('row', 'col')), may hold values from -6 to 6
- valence_energy: float32 [256], P(('row', 'col')), may hold values from -8 to -0.5
- conduction_energy: float32 [256], P(('row', 'col')), may hold values from 0.5 to 8
- pair_valence: int32 [128, 4], P(('row', 'col')), may hold values from 0 to 1
- pair_conduction: int32 [128, 4], P(('row', 'col')), may hold values from 0 to 1
- pair_count: int32 [128], replicated, may hold values from 1 to 4, 256 in all
- stick_perm: int32 [160], replicated, may hold values from 0 to 159, each once
Outputs:
- response: float32 [20480, 20480], P('row', 'col')
The draws below stay inside these ranges and needn't reach their ends.
Inputs may be any that keep to these rules, and one draw needn't show every extreme that they name: `pair_count`: the numbers sum to 256 and the largest is 4. `stick_perm`: A permutation of the box sticks.
All inputs are finite; a program needn't handle non-finite values.
Results may differ from the reference program's by a relative error of at most 0.0003.
Values sent between devices are 32-bit elements; how exact they have to be, the bound alone decides.
No kernel may reach another device: no remote copies, remote signals or barrier semaphores. Data moves between devices by JAX's collectives and lax.ppermute only.
A program may use at most 128 MiB of HBM per device.

```python
import math
import jax
import jax.numpy as jnp
import numpy as np
from jax import lax

NG = 96
KX = 10
KY = 16
KZ = 64
VB_DEV = 2
CB_DEV = 2
CAP = 4
NSTICK = 160
NPW = 20480
PAIRS = 256
N_ROW = 8
N_COL = 16


def set_ends(values, rng, smallest, high):
    longest = values.shape.index(max(values.shape))
    spots = []
    for shift in (0, 1):
        where = [jax.random.randint(jax.random.fold_in(rng, axis), (), 0, length) for axis, length in enumerate(values.shape)]
        where[longest] = (where[longest] + shift) % values.shape[longest]
        spots.append(tuple(where))
    return values.at[spots[0]].set(smallest).at[spots[1]].set(high)


def steps_of(stream_key, dims, shards, low, high):
    loudness, own = 1.0, jax.random.fold_in(stream_key, 6)
    for position, shards_of in shards:
        steps = jnp.exp(jax.random.uniform(jax.random.fold_in(own, position), (shards_of,), jnp.float32, low / len(shards), high / len(shards)))
        loudness = loudness * jnp.repeat(steps, dims[position] // shards_of).reshape([-1 if axis == position else 1 for axis in range(len(dims))])
    return loudness


def length_profile(count, total, reach, lean):
    weights = [(1 << 20) // math.isqrt(rank ** lean) + 1 for rank in range(2, count + 1)]
    rest, holding = total - reach - (count - 1), [1] * (count - 1)
    while rest > 0:
        movable = [i for i in range(count - 1) if holding[i] < reach]
        whole, budget = sum([weights[i] for i in movable]), rest
        for i in movable:
            more = min(reach - holding[i], max(1, budget * weights[i] // whole), rest)
            holding[i] = holding[i] + more
            rest = rest - more
    return np.array([reach] + holding)


def ragged(key, amount, total, reach, slope):
    if amount == 2:
        one = jax.random.randint(key, (), max(1, total - reach), min(reach, total - 1) + 1)
        return jnp.stack([one, total - one])
    sizes = jnp.asarray(length_profile(amount, total, reach, slope), jnp.int32)
    twos = (amount - 1) // 2
    donor, taker = sizes[1:1 + 2 * twos:2], sizes[2:2 + 2 * twos:2]
    room = jnp.minimum(donor - 1, reach - taker)
    passed = jax.random.randint(jax.random.fold_in(key, 1), (twos,), 0, 1 << 20) % (room + 1)
    sizes = sizes.at[1:1 + 2 * twos:2].set(donor - passed).at[2:2 + 2 * twos:2].set(taker + passed)
    return sizes[jax.random.permutation(jax.random.fold_in(key, 2), amount)]


def centred(own_key, dims, spread, reach, shards=(), held_as=jnp.bfloat16):
    level = steps_of(own_key, dims, shards, -0.22, 0.18) if shards else 1.0
    entries = jax.random.normal(own_key, dims, jnp.float32) * spread * level
    return jnp.minimum(jnp.maximum(entries, -reach), reach).astype(held_as)


def setup_inputs(seed: int = 0) -> dict:
    arg_keys = jax.random.split(jax.random.key(seed), 9)
    return {
        "valence_bands": centred(arg_keys[0], (N_ROW * N_COL * VB_DEV, NG, NG * NG), 1.0, 6.0, ((0, 128),)),
        "conduction_bands": centred(arg_keys[1], (N_ROW * N_COL * CB_DEV, NG, NG * NG), 1.0, 6.0, ((0, 128),)),
        "valence_energy": jnp.clip(-8.0 + 7.5 * jax.random.uniform(arg_keys[2], (N_ROW * N_COL * VB_DEV,), jnp.float32) ** steps_of(arg_keys[2], (N_ROW * N_COL * VB_DEV,), ((0, 128),), -0.2, 0.2), -8.0, -0.5),
        "conduction_energy": jnp.clip(0.5 + 7.5 * jax.random.uniform(arg_keys[3], (N_ROW * N_COL * CB_DEV,), jnp.float32) ** steps_of(arg_keys[3], (N_ROW * N_COL * CB_DEV,), ((0, 128),), -0.2, 0.2), 0.5, 8.0),
        "pair_valence": set_ends(jax.random.randint(arg_keys[4], (N_ROW * N_COL, CAP), 0, VB_DEV), jax.random.fold_in(arg_keys[4], 1), 0, VB_DEV - 1).astype(jnp.int32),
        "pair_conduction": set_ends(jax.random.randint(arg_keys[5], (N_ROW * N_COL, CAP), 0, CB_DEV), jax.random.fold_in(arg_keys[5], 1), 0, CB_DEV - 1).astype(jnp.int32),
        "pair_count": ragged(arg_keys[6], N_ROW * N_COL, PAIRS, CAP, 2).astype(jnp.int32),
        "stick_perm": jax.random.permutation(arg_keys[7], NSTICK).astype(jnp.int32),
    }


def coefficients(product):
    spectrum = jnp.fft.fftn(product)
    kept_part = spectrum[1:KX + 1, :KY, :KZ]
    stacked = jnp.concatenate([jnp.real(kept_part), jnp.imag(kept_part)], axis=-1) * (NG ** -1.5)
    return stacked.reshape(KX * KY, 2 * KZ)


def reference(valence_bands, conduction_bands, valence_energy, conduction_energy, pair_valence, pair_conduction, pair_count, stick_perm):
    offsets = (jnp.cumsum(pair_count) - pair_count).astype(jnp.int32)
    pair_order = jnp.arange(PAIRS, dtype=jnp.int32)
    before = offsets[None, :] <= pair_order[:, None]
    source = (jnp.sum(before.astype(jnp.int32), axis=1) - 1).astype(jnp.int32)
    within = (pair_order - jnp.max(jnp.where(before, offsets[None, :], 0), axis=1)).astype(jnp.int32)
    valence_row = (source * VB_DEV + pair_valence[source, within]).astype(jnp.int32)
    conduction_row = (source * CB_DEV + pair_conduction[source, within]).astype(jnp.int32)
    weight = -1.0 / (conduction_energy[conduction_row] - valence_energy[valence_row])

    def one_pair(band_rows):
        left_band = valence_bands[band_rows[0]].astype(jnp.float32).reshape(NG, NG, NG)
        right_band = conduction_bands[band_rows[1]].astype(jnp.float32).reshape(NG, NG, NG)
        sticks = coefficients(left_band * right_band)
        return sticks[stick_perm].reshape(NPW)

    density = lax.map(one_pair, (valence_row, conduction_row))
    weighted = density * weight[:, None]
    return lax.dot_general(weighted, density, (((0,), (0,)), ((), ())), precision=lax.Precision.HIGHEST, preferred_element_type=jnp.float32)
```

```python
import math

import jax
import jax.numpy as jnp
import numpy as np
from jax import lax
from jax.experimental import pallas as pl
from jax.experimental.pallas import tpu as pltpu
from jax.sharding import Mesh, PartitionSpec as P

NG = 96
KX = 10
KY = 16
KZ = 64
CAP = 4
NSTICK = 160
LANES = 128
NY, NCORE, NX, NZ = 4, 2, 4, 4
DEVICES = 128
AXIS = {"y": NY, "core": NCORE, "x": NX, "z": NZ}

YL = 4
NB = NG // YL
Q = YL * NG
GROWS = 24
BCHUNK = 4
STEPS = NB // BCHUNK
CHUNK = BCHUNK * Q
F32 = jnp.float32
BF16 = jnp.bfloat16


def split_np(table):
    table = np.asarray(table, np.float32)
    high = table.astype(jnp.bfloat16)
    low = (table - high.astype(np.float32)).astype(jnp.bfloat16)
    return high, low


def tables():
    x = np.arange(NG)
    gx = np.arange(1, KX + 1)
    angle = 2 * math.pi / NG * ((gx[:, None] * x[None, :]) % NG)
    factor = np.zeros((GROWS, NG))
    factor[:KX] = np.cos(angle)
    factor[KX : 2 * KX] = -np.sin(angle)
    high, low = split_np(factor)
    x_table = np.concatenate(
        [np.concatenate([high, high], 1), np.concatenate([low, low], 1)], 0
    )
    b = np.arange(NB)
    gy = np.arange(KY)
    phi = 2 * math.pi / NB * ((gy[:, None] * b[None, :]) % NB)
    mix = np.zeros((2, KX, KY, NB, GROWS))
    for i in range(KX):
        mix[0, i, :, :, i] = np.cos(phi)
        mix[0, i, :, :, KX + i] = np.sin(phi)
        mix[1, i, :, :, KX + i] = np.cos(phi)
        mix[1, i, :, :, i] = -np.sin(phi)
    mix_high, mix_low = split_np(mix.reshape(2 * NSTICK, NB * GROWS))
    q = np.arange(Q)
    twist = 2 * math.pi / NG * (gy[:, None] * (q // NG)[None, :])
    twist = np.stack([np.cos(twist), np.sin(twist)]).astype(np.float32)
    gz = np.arange(KZ)
    theta = 2 * math.pi / NG * (((q % NG)[:, None] * gz[None, :]) % NG)
    cosine, sine = np.cos(theta), np.sin(theta)
    z_table = np.concatenate(
        [np.concatenate([cosine, -sine], 1), np.concatenate([sine, cosine], 1)], 0
    )
    z_high, z_low = split_np(z_table)
    return x_table, mix_high, mix_low, twist, z_high, z_low


def split(value):
    high = value.astype(BF16)
    low = (value - high.astype(F32)).astype(BF16)
    return high, low


def dot(left, right):
    return jnp.dot(left, right, preferred_element_type=F32)


def lane_group(rows):
    return lax.broadcasted_iota(jnp.int32, (rows, LANES), 1) // 32


def pack(sticks_2d, out, slots, rows_per_dest):
    half = rows_per_dest // 2
    units = [(k, s) for k in slots for s in range(5)]
    for q in range(4):
        for row in range(half):
            held = units[4 * row : 4 * row + 4]
            parts = []
            for k, s in held:
                parts.append(sticks_2d[pl.ds(8 * s + k, 32, stride=40), :])
            total = jnp.zeros((32, LANES), F32)
            group = lane_group(32)
            for g, part in enumerate(parts):
                shift = (32 * (g - q)) % LANES
                moved = pltpu.roll(part, shift, 1) if shift else part
                total = jnp.where(group == g, moved, total)
            out[pl.ds(rows_per_dest * q + row, 32, stride=4 * rows_per_dest), :] = total
            for h in range(2):
                parts = []
                for k, s in held:
                    parts.append(
                        sticks_2d[pl.ds(8 * (5 * h + s) + k, 16, stride=80), :]
                    )
                total = jnp.zeros((16, LANES), F32)
                group = lane_group(16)
                for g, part in enumerate(parts):
                    shift = (32 * (g - q)) % LANES
                    moved = pltpu.roll(part, shift, 1) if shift else part
                    total = jnp.where(group == g, moved, total)
                start = rows_per_dest * (32 * q + 16 * h) + half + row
                out[pl.ds(start, 16, stride=rows_per_dest), :] = total


def transform_kernel(
    slot_v,
    slot_c,
    perm,
    energy_v,
    energy_c,
    v_ref,
    c_ref,
    x_table,
    mix_high,
    mix_low,
    twist,
    z_high,
    z_low,
    out_first,
    out_rest,
    zh,
    zl,
    natural,
    ordered,
):
    step = pl.program_id(0)
    for k in range(CAP):
        left = v_ref[slot_v[0, k]].astype(F32)
        right = c_ref[slot_c[0, k]].astype(F32)
        high, low = split(left * right)
        x_part = dot(x_table[...], jnp.concatenate([high, low], 0))
        x_part = x_part[:GROWS] + x_part[GROWS:]
        for pair in range(BCHUNK // 2):
            two = jnp.concatenate(
                [
                    x_part[:, Q * (2 * pair) : Q * (2 * pair + 1)],
                    x_part[:, Q * (2 * pair + 1) : Q * (2 * pair + 2)],
                ],
                0,
            )
            high, low = split(two)
            row = pl.multiple_of(step * (BCHUNK * GROWS) + 2 * GROWS * pair, 16)
            zh[pl.ds(row, 2 * GROWS), Q * k : Q * (k + 1)] = high
            zl[pl.ds(row, 2 * GROWS), Q * k : Q * (k + 1)] = low

    @pl.when(step == STEPS - 1)
    def _():
        turn_c = twist[0][None]
        turn_s = twist[1][None]
        for k in range(CAP):
            z_slot_high = zh[:, Q * k : Q * (k + 1)]
            z_slot_low = zl[:, Q * k : Q * (k + 1)]
            mixed = (
                dot(mix_high[...], z_slot_high)
                + dot(mix_high[...], z_slot_low)
                + dot(mix_low[...], z_slot_high)
            )
            real = mixed[:NSTICK].reshape(KX, KY, Q)
            imag = mixed[NSTICK:].reshape(KX, KY, Q)
            turned_real = (real * turn_c + imag * turn_s).reshape(NSTICK, Q)
            turned_imag = (imag * turn_c - real * turn_s).reshape(NSTICK, Q)
            high, low = split(jnp.concatenate([turned_real, turned_imag], 1))
            value = (
                dot(high, z_high[...]) + dot(low, z_high[...]) + dot(high, z_low[...])
            )
            gap = energy_c[slot_c[0, k]] - energy_v[slot_v[0, k]]
            gap = jnp.full((1, LANES), gap, F32)
            value = value * (jnp.sqrt(1.0 / gap) * NG ** (-1.5))
            natural[pl.ds(k, NSTICK, stride=8), :] = value

        def move(s, carry):
            source = pl.multiple_of(8 * perm[s], 8)
            target = pl.multiple_of(8 * s, 8)
            ordered[pl.ds(target, 8), :] = natural[pl.ds(source, 8), :]
            return carry

        lax.fori_loop(0, NSTICK, move, 0, unroll=8)
        pack(ordered, out_first, (0,), 4)
        pack(ordered, out_rest, (1, 2, 3), 8)


def transform(v, c, ev, ec, slot_v, slot_c, perm):
    x_table, mix_high, mix_low, twist, z_high, z_low = tables()
    whole = lambda a: pl.BlockSpec(a.shape, lambda i, *_: (0,) * a.ndim)
    consts = [jnp.asarray(t) for t in (x_table, mix_high, mix_low, twist, z_high, z_low)]
    bands = pl.BlockSpec((2, NG, CHUNK), lambda i, *_: (0, 0, i))
    return pl.pallas_call(
        transform_kernel,
        name="transform",
        out_shape=(
            jax.ShapeDtypeStruct((4 * DEVICES, LANES), F32),
            jax.ShapeDtypeStruct((8 * DEVICES, LANES), F32),
        ),
        grid_spec=pltpu.PrefetchScalarGridSpec(
            num_scalar_prefetch=5,
            grid=(STEPS,),
            in_specs=[bands, bands] + [whole(t) for t in consts],
            out_specs=(
                pl.BlockSpec((4 * DEVICES, LANES), lambda i, *_: (0, 0)),
                pl.BlockSpec((8 * DEVICES, LANES), lambda i, *_: (0, 0)),
            ),
            scratch_shapes=[
                pltpu.VMEM((NB * GROWS, CAP * Q), BF16),
                pltpu.VMEM((NB * GROWS, CAP * Q), BF16),
                pltpu.VMEM((8 * NSTICK, LANES), F32),
                pltpu.VMEM((8 * NSTICK, LANES), F32),
            ],
        ),
        cost_estimate=pl.CostEstimate(
            flops=2_000_000_000, bytes_accessed=9_000_000, transcendentals=0
        ),
    )(slot_v, slot_c, perm, ev, ec, v, c, *consts)


def first_kernel(x_ref, row_out, col_out):
    for part, out in ((0, row_out), (2, col_out)):
        out[:128, :] = x_ref[pl.ds(part, DEVICES, stride=4), :].T
        out[128:, :] = x_ref[pl.ds(part + 1, DEVICES, stride=4), :].T[:32]


def first_pieces(received):
    shape = jax.ShapeDtypeStruct((160, LANES), F32)
    return pl.pallas_call(
        first_kernel,
        name="first_pieces",
        out_shape=(shape, shape),
        cost_estimate=pl.CostEstimate(
            flops=100_000, bytes_accessed=600_000, transcendentals=0
        ),
    )(received)


def rest_kernel(count_ref, x_ref, row_out, col_out):
    counts = jnp.broadcast_to(count_ref[...], (DEVICES, LANES)) - 1
    device = lax.broadcasted_iota(jnp.int32, (DEVICES, LANES), 0)
    lane = lax.broadcasted_iota(jnp.int32, (DEVICES, LANES), 1)
    offset = jnp.sum(jnp.where(lane < device, counts, 0), axis=1, keepdims=True)
    own = jnp.sum(jnp.where(lane == device, counts, 0), axis=1, keepdims=True)
    chosen = []
    for k in range(CAP - 1):
        hit = jnp.logical_and(lane == offset + k, k < own)
        chosen.append(jnp.where(hit, 1.0, 0.0).astype(BF16))
    chosen = jnp.concatenate(chosen + chosen, 0)
    for part, out in ((0, row_out), (4, col_out)):
        turned = [x_ref[pl.ds(part + i, DEVICES, stride=8), :].T for i in range(4)]
        flat = jnp.concatenate(turned, 0)
        wide = jnp.concatenate([flat[160 * k : 160 * (k + 1)] for k in range(3)], 1)
        high, low = split(wide)
        out[...] = dot(jnp.concatenate([high, low], 1), chosen)


def rest_pieces(counts, received):
    shape = jax.ShapeDtypeStruct((160, LANES), F32)
    return pl.pallas_call(
        rest_kernel,
        name="rest_pieces",
        out_shape=(shape, shape),
        cost_estimate=pl.CostEstimate(
            flops=60_000_000, bytes_accessed=800_000, transcendentals=0
        ),
    )(counts, received)


def product_kernel(where, *refs):
    first = refs[0:4]
    rest = refs[4:8]
    columns = refs[8:12]
    out, a3, b_flat, b3 = refs[12:]
    step = pl.program_id(0)
    y, core, z = where[1], where[2], where[3]

    @pl.when(step == 0)
    def _():
        for half in range(2):
            for other in range(2):
                source = columns[2 * half + other]
                base = 640 * ((core + other) % 2)
                for m in range(4):
                    there = (y + 4 - m) % 4
                    for s in range(5):
                        row = pl.multiple_of(base + 128 * s + 32 * there, 32)
                        b_flat[pl.ds(row, 32), 128 * half : 128 * half + 128] = source[
                            m, 32 * s : 32 * s + 32, :
                        ]
        for i in range(10):
            turned = -b_flat[128 * i : 128 * i + 128, :].T
            high, low = split(turned)
            b3[0:256, 128 * i : 128 * i + 128] = high
            b3[256:512, 128 * i : 128 * i + 128] = low
            b3[512:768, 128 * i : 128 * i + 128] = high

    for k in range(4):

        @pl.when(step == k)
        def _():
            for m in range(4):
                there = (z + 4 - m) % 4
                for s in range(5):
                    row = pl.multiple_of(128 * s + 32 * there, 32)
                    for half, source in ((0, first[k].at[m]), (1, rest[m].at[k])):
                        high, low = split(source[32 * s : 32 * s + 32, :])
                        lane = 128 * half
                        a3[pl.ds(row, 32), lane : lane + 128] = high
                        a3[pl.ds(row, 32), 256 + lane : 384 + lane] = high
                        a3[pl.ds(row, 32), 512 + lane : 640 + lane] = low

    for j in range(5):
        out[:, 256 * j : 256 * j + 256] = dot(a3[...], b3[:, 256 * j : 256 * j + 256])


def response_block(where, first, rest, columns):
    gathered = [*first, *rest, *columns]
    whole = lambda a: pl.BlockSpec(a.shape, lambda i, *_: (0,) * a.ndim)
    return pl.pallas_call(
        product_kernel,
        name="response",
        out_shape=jax.ShapeDtypeStruct((2560, 1280), F32),
        grid_spec=pltpu.PrefetchScalarGridSpec(
            num_scalar_prefetch=1,
            grid=(4,),
            in_specs=[whole(a) for a in gathered],
            out_specs=pl.BlockSpec((640, 1280), lambda i, w: ((w[0] + 4 - i) % 4, 0)),
            scratch_shapes=[
                pltpu.VMEM((640, 768), BF16),
                pltpu.VMEM((1280, 256), F32),
                pltpu.VMEM((768, 1280), BF16),
            ],
        ),
        cost_estimate=pl.CostEstimate(
            flops=5_000_000_000, bytes_accessed=17_000_000, transcendentals=0
        ),
    )(where, *gathered)


def shift(value, axis, k):
    n = AXIS[axis]
    return lax.ppermute(value, axis, [(i, (i + k) % n) for i in range(n)])


def gather(value, axis):
    return [value] + [shift(value, axis, k) for k in range(1, AXIS[axis])]


def exchange(value, rows):
    value = value.reshape(DEVICES, rows, LANES)
    value = lax.all_to_all(
        value, ("y", "core", "x", "z"), split_axis=0, concat_axis=0, tiled=True
    )
    return value.reshape(DEVICES * rows, LANES)


def body(v, c, ev, ec, slot_v, slot_c, count, perm):
    to_first, to_rest = transform(v, c, ev, ec, slot_v, slot_c, perm)
    got_first = exchange(to_first, 4)
    got_rest = exchange(to_rest, 8)
    row_first, col_first = first_pieces(got_first)
    row_rest, col_rest = rest_pieces(count.reshape(1, DEVICES), got_rest)
    first = gather(jnp.stack(gather(row_first, "z")), "x")
    rest = gather(jnp.stack(gather(row_rest, "x")), "z")
    columns = []
    for piece in (col_first, col_rest):
        mine = jnp.stack(gather(piece, "y"))
        columns += [mine, shift(mine, "core", 1)]
    where = jnp.stack([lax.axis_index(a) for a in ("x", "y", "core", "z")])
    return response_block(where.astype(jnp.int32), first, rest, columns)


def solution(mesh):
    fine = Mesh(mesh.devices.reshape(NY, NCORE, NX, NZ), ("y", "core", "x", "z"))
    every = ("y", "core", "x", "z")
    return jax.shard_map(
        body,
        mesh=fine,
        in_specs=(
            P(every, None, None),
            P(every, None, None),
            P(every),
            P(every),
            P(every, None),
            P(every, None),
            P(),
            P(),
        ),
        out_specs=P(("y", "core"), ("x", "z")),
        check_vma=False,
    )
```

```python
import math

import jax
import jax.numpy as jnp
import numpy as np
from jax import lax
from jax.experimental import pallas as pl
from jax.experimental.pallas import tpu as pltpu
from jax.sharding import Mesh, PartitionSpec as P

NG = 96
KX = 10
KY = 16
KZ = 64
CAP = 4
NSTICK = 160
LANES = 128
NY, NCORE, NX, NZ = 4, 2, 4, 4
DEVICES = 128
PAIRS = 256
AXIS = {"y": NY, "core": NCORE, "x": NX, "z": NZ}

YL = 4
NB = NG // YL
Q = YL * NG
GROWS = 24
BCHUNK = 4
STEPS = NB // BCHUNK
CHUNK = BCHUNK * Q
F32 = jnp.float32
BF16 = jnp.bfloat16


def split_np(table):
    table = np.asarray(table, np.float32)
    high = table.astype(jnp.bfloat16)
    low = (table - high.astype(np.float32)).astype(jnp.bfloat16)
    return high, low


def tables():
    x = np.arange(NG)
    gx = np.arange(1, KX + 1)
    angle = 2 * math.pi / NG * ((gx[:, None] * x[None, :]) % NG)
    factor = np.zeros((GROWS, NG))
    factor[:KX] = np.cos(angle)
    factor[KX : 2 * KX] = -np.sin(angle)
    high, low = split_np(factor)
    x_table = np.concatenate(
        [np.concatenate([high, high], 1), np.concatenate([low, low], 1)], 0
    )
    b = np.arange(NB)
    gy = np.arange(KY)
    phi = 2 * math.pi / NB * ((gy[:, None] * b[None, :]) % NB)
    mix = np.zeros((2, KX, KY, NB, GROWS))
    for i in range(KX):
        mix[0, i, :, :, i] = np.cos(phi)
        mix[0, i, :, :, KX + i] = np.sin(phi)
        mix[1, i, :, :, KX + i] = np.cos(phi)
        mix[1, i, :, :, i] = -np.sin(phi)
    mix_high, mix_low = split_np(mix.reshape(2 * NSTICK, NB * GROWS))
    q = np.arange(Q)
    twist = 2 * math.pi / NG * (gy[:, None] * (q // NG)[None, :])
    twist = np.stack([np.cos(twist), np.sin(twist)]).astype(np.float32)
    gz = np.arange(KZ)
    theta = 2 * math.pi / NG * (((q % NG)[:, None] * gz[None, :]) % NG)
    cosine, sine = np.cos(theta), np.sin(theta)
    z_table = np.concatenate(
        [np.concatenate([cosine, -sine], 1), np.concatenate([sine, cosine], 1)], 0
    )
    z_high, z_low = split_np(z_table)
    return x_table, mix_high, mix_low, twist, z_high, z_low


def split(value):
    high = value.astype(BF16)
    low = (value - high.astype(F32)).astype(BF16)
    return high, low


def dot(left, right):
    return jnp.dot(left, right, preferred_element_type=F32)


def lane_group(rows):
    return lax.broadcasted_iota(jnp.int32, (rows, LANES), 1) // 32


def quarters(sticks_2d, q, start, count, stride):
    total = None
    for k in range(CAP):
        part = sticks_2d[pl.ds(8 * start + k, count, stride=8 * stride), :]
        turn = (32 * (k - q)) % LANES
        moved = pltpu.roll(part, turn, 1) if turn else part
        total = moved if total is None else jnp.where(lane_group(count) == k, moved, total)
    return total


def pack(sticks_2d, out):
    for q in range(4):
        for s in range(5):
            value = quarters(sticks_2d, q, s, 32, 5)
            for y in range(4):
                start = 10 * (32 * y + q) + s
                out[pl.ds(start, 4, stride=40), :] = value[8 * y : 8 * y + 4]
                start = 10 * (32 * y + 16 + 4 * q) + s
                out[pl.ds(start, 4, stride=10), :] = value[8 * y + 4 : 8 * y + 8]
            for h in range(2):
                out[pl.ds(10 * (32 * q + 16 * h) + 5 + s, 16, stride=10), :] = quarters(
                    sticks_2d, q, 5 * h + s, 16, 10
                )


def transform_kernel(
    slot_v,
    slot_c,
    perm,
    energy_v,
    energy_c,
    v_ref,
    c_ref,
    x_table,
    mix_high,
    mix_low,
    twist,
    z_high,
    z_low,
    out,
    zh,
    zl,
    natural,
    ordered,
):
    step = pl.program_id(0)
    for k in range(CAP):
        left = v_ref[slot_v[0, k]].astype(F32)
        right = c_ref[slot_c[0, k]].astype(F32)
        high, low = split(left * right)
        x_part = dot(x_table[...], jnp.concatenate([high, low], 0))
        x_part = x_part[:GROWS] + x_part[GROWS:]
        for pair in range(BCHUNK // 2):
            two = jnp.concatenate(
                [
                    x_part[:, Q * (2 * pair) : Q * (2 * pair + 1)],
                    x_part[:, Q * (2 * pair + 1) : Q * (2 * pair + 2)],
                ],
                0,
            )
            high, low = split(two)
            row = pl.multiple_of(step * (BCHUNK * GROWS) + 2 * GROWS * pair, 16)
            zh[pl.ds(row, 2 * GROWS), Q * k : Q * (k + 1)] = high
            zl[pl.ds(row, 2 * GROWS), Q * k : Q * (k + 1)] = low

    @pl.when(step == STEPS - 1)
    def _():
        turn_c = twist[0][None]
        turn_s = twist[1][None]
        for k in range(CAP):
            z_slot_high = zh[:, Q * k : Q * (k + 1)]
            z_slot_low = zl[:, Q * k : Q * (k + 1)]
            mixed = (
                dot(mix_high[...], z_slot_high)
                + dot(mix_high[...], z_slot_low)
                + dot(mix_low[...], z_slot_high)
            )
            real = mixed[:NSTICK].reshape(KX, KY, Q)
            imag = mixed[NSTICK:].reshape(KX, KY, Q)
            turned_real = (real * turn_c + imag * turn_s).reshape(NSTICK, Q)
            turned_imag = (imag * turn_c - real * turn_s).reshape(NSTICK, Q)
            high, low = split(jnp.concatenate([turned_real, turned_imag], 1))
            value = (
                dot(high, z_high[...]) + dot(low, z_high[...]) + dot(high, z_low[...])
            )
            gap = energy_c[slot_c[0, k]] - energy_v[slot_v[0, k]]
            gap = jnp.full((1, LANES), gap, F32)
            value = value * (jnp.sqrt(1.0 / gap) * NG ** (-1.5))
            natural[pl.ds(k, NSTICK, stride=8), :] = value

        def move(s, carry):
            source = pl.multiple_of(8 * perm[s], 8)
            target = pl.multiple_of(8 * s, 8)
            ordered[pl.ds(target, 8), :] = natural[pl.ds(source, 8), :]
            return carry

        lax.fori_loop(0, NSTICK, move, 0, unroll=8)
        pack(ordered, out)


def transform(v, c, ev, ec, slot_v, slot_c, perm):
    x_table, mix_high, mix_low, twist, z_high, z_low = tables()
    whole = lambda a: pl.BlockSpec(a.shape, lambda i, *_: (0,) * a.ndim)
    consts = [jnp.asarray(t) for t in (x_table, mix_high, mix_low, twist, z_high, z_low)]
    bands = pl.BlockSpec((2, NG, CHUNK), lambda i, *_: (0, 0, i))
    return pl.pallas_call(
        transform_kernel,
        name="transform",
        out_shape=jax.ShapeDtypeStruct((10 * DEVICES, LANES), F32),
        grid_spec=pltpu.PrefetchScalarGridSpec(
            num_scalar_prefetch=5,
            grid=(STEPS,),
            in_specs=[bands, bands] + [whole(t) for t in consts],
            out_specs=pl.BlockSpec((10 * DEVICES, LANES), lambda i, *_: (0, 0)),
            scratch_shapes=[
                pltpu.VMEM((NB * GROWS, CAP * Q), BF16),
                pltpu.VMEM((NB * GROWS, CAP * Q), BF16),
                pltpu.VMEM((8 * NSTICK, LANES), F32),
                pltpu.VMEM((8 * NSTICK, LANES), F32),
            ],
        ),
        cost_estimate=pl.CostEstimate(
            flops=4_000_000_000,
            bytes_accessed=9_000_000,
            transcendentals=0,
        ),
    )(slot_v, slot_c, perm, ev, ec, v, c, *consts)


def pieces_kernel(count_ref, x_ref, row_out, col_out):
    counts = jnp.broadcast_to(count_ref[...], (DEVICES, LANES))
    device = lax.broadcasted_iota(jnp.int32, (DEVICES, LANES), 0)
    lane = lax.broadcasted_iota(jnp.int32, (DEVICES, LANES), 1)
    offset = jnp.sum(jnp.where(lane < device, counts, 0), axis=1, keepdims=True)
    own = jnp.sum(jnp.where(lane == device, counts, 0), axis=1, keepdims=True)
    pair = lax.broadcasted_iota(jnp.int32, (DEVICES, PAIRS), 1)
    chosen = []
    for k in range(CAP):
        hit = jnp.logical_and(pair == offset + k, k < own)
        chosen.append(jnp.where(hit, 1.0, 0.0).astype(BF16))
    chosen = jnp.concatenate(chosen + chosen, 0)
    wide = []
    for s in range(10):
        turned = x_ref[pl.ds(s, DEVICES, stride=10), :].T
        wide.append(
            jnp.concatenate([turned[32 * k : 32 * k + 32] for k in range(CAP)], 1)
        )
    high, low = split(jnp.concatenate(wide, 0))
    total = dot(jnp.concatenate([high, low], 1), chosen)
    row_out[...] = total[:160]
    col_out[...] = total[160:]


def pieces(count, received):
    shape = jax.ShapeDtypeStruct((160, PAIRS), F32)
    return pl.pallas_call(
        pieces_kernel,
        name="pieces",
        compiler_params=pltpu.CompilerParams(vmem_limit_bytes=12 << 20),
        out_shape=(shape, shape),
        cost_estimate=pl.CostEstimate(
            flops=180_000_000, bytes_accessed=1_000_000, transcendentals=0
        ),
    )(count, received)


def columns_kernel(where, mine, theirs, out, flat):
    y, core = where[1], where[2]
    for other, source in enumerate((mine, theirs)):
        base = 640 * ((core + other) % 2)
        for m in range(4):
            there = (y + 4 - m) % 4
            for s in range(5):
                row = pl.multiple_of(base + 128 * s + 32 * there, 32)
                flat[pl.ds(row, 32), :] = source[m, 32 * s : 32 * s + 32, :]
    for i in range(10):
        high, low = split(-flat[128 * i : 128 * i + 128, :].T)
        out[0:256, 128 * i : 128 * i + 128] = high
        out[256:512, 128 * i : 128 * i + 128] = low
        out[512:768, 128 * i : 128 * i + 128] = high


def columns(where, mine, theirs):
    vmem = pl.BlockSpec(memory_space=pltpu.VMEM)
    return pl.pallas_call(
        columns_kernel,
        name="columns",
        compiler_params=pltpu.CompilerParams(vmem_limit_bytes=16 << 20),
        out_shape=jax.ShapeDtypeStruct((3 * PAIRS, 1280), BF16),
        in_specs=[pl.BlockSpec(memory_space=pltpu.SMEM), vmem, vmem],
        out_specs=vmem,
        scratch_shapes=[pltpu.VMEM((1280, PAIRS), F32)],
        cost_estimate=pl.CostEstimate(
            flops=2_000_000, bytes_accessed=3_000_000, transcendentals=0
        ),
    )(where, mine, theirs)


def product_kernel(where, *refs):
    gathered = refs[0:4]
    b3, out, a3 = refs[4:]
    step = pl.program_id(0)
    part = pl.program_id(1)
    for k in range(4):

        @pl.when(jnp.logical_and(step == k, part == 0))
        def _():
            for m in range(4):
                there = (where[3] + 4 - m) % 4
                for s in range(5):
                    row = pl.multiple_of(128 * s + 32 * there, 32)
                    high, low = split(gathered[k][m, 32 * s : 32 * s + 32, :])
                    a3[pl.ds(row, 32), 0:256] = high
                    a3[pl.ds(row, 32), 256:512] = high
                    a3[pl.ds(row, 32), 512:768] = low

    lane = pl.multiple_of(640 * part, 640)
    out[...] = dot(a3[...], b3[:, pl.ds(lane, 640)])


def response_block(where, gathered, b3):
    vmem = pl.BlockSpec(memory_space=pltpu.VMEM)
    return pl.pallas_call(
        product_kernel,
        name="response",
        compiler_params=pltpu.CompilerParams(vmem_limit_bytes=24 << 20),
        out_shape=jax.ShapeDtypeStruct((2560, 1280), F32),
        grid_spec=pltpu.PrefetchScalarGridSpec(
            num_scalar_prefetch=1,
            grid=(4, 2),
            in_specs=[vmem] * 5,
            out_specs=pl.BlockSpec(
                (640, 640), lambda i, j, w: ((w[0] + 4 - i) % 4, j)
            ),
            scratch_shapes=[pltpu.VMEM((640, 768), BF16)],
        ),
        cost_estimate=pl.CostEstimate(
            flops=5_000_000_000, bytes_accessed=17_000_000, transcendentals=0
        ),
    )(where, *gathered, b3)


def shift(value, axis, k):
    n = AXIS[axis]
    return lax.ppermute(value, axis, [(i, (i + k) % n) for i in range(n)])


def gather(value, axis):
    return [value] + [shift(value, axis, k) for k in range(1, AXIS[axis])]


def plane_gather(value, stage):
    got = [value]
    for k in range(1, 4):
        pairs = []
        for core in range(NCORE):
            for x in range(NX):
                for z in range(NZ):
                    if core == stage:
                        to = (x, (z + k) % NZ)
                    else:
                        to = ((x + k) % NX, z)
                    pairs.append(
                        (16 * core + 4 * x + z, 16 * core + 4 * to[0] + to[1])
                    )
        got.append(lax.ppermute(value, ("core", "x", "z"), pairs))
    return got


def exchange(value):
    value = value.reshape(DEVICES, 10, 1, LANES)
    value = lax.all_to_all(
        value, ("y", "core", "x", "z"), split_axis=0, concat_axis=0, tiled=True
    )
    return value.reshape(DEVICES * 10, LANES)


def body(v, c, ev, ec, slot_v, slot_c, count, perm):
    packed = transform(v, c, ev, ec, slot_v, slot_c, perm)
    row, column = pieces(count.reshape(1, DEVICES), exchange(packed))
    x, y, core, z = (lax.axis_index(a) for a in ("x", "y", "core", "z"))
    where = jnp.stack([jnp.where(core == 0, x, z), y, core, jnp.where(core == 0, z, x)])
    where = where.astype(jnp.int32)
    gathered = plane_gather(jnp.stack(plane_gather(row, 0)), 1)
    mine = jnp.stack(gather(column, "y"))
    b3 = columns(where, mine, shift(mine, "core", 1))
    return response_block(where, gathered, b3)


def solution(mesh):
    fine = Mesh(mesh.devices.reshape(NY, NCORE, NX, NZ), ("y", "core", "x", "z"))
    every = ("y", "core", "x", "z")
    return jax.shard_map(
        body,
        mesh=fine,
        in_specs=(
            P(every, None, None),
            P(every, None, None),
            P(every),
            P(every),
            P(every, None),
            P(every, None),
            P(),
            P(),
        ),
        out_specs=P(("y", "core"), ("x", "z")),
        check_vma=False,
    )
```

```python
import functools
import math

import jax
import jax.numpy as jnp
import numpy as np
from jax import lax
from jax.experimental import pallas as pl
from jax.experimental.pallas import tpu as pltpu
from jax.sharding import Mesh, PartitionSpec as P

NG = 96
KX = 10
KY = 16
KZ = 64
CAP = 4
NSTICK = 160
LANES = 128
NY, NCORE, NX, NZ = 4, 2, 4, 4
DEVICES = 128
PAIRS = 256
AXIS = {"y": NY, "core": NCORE, "x": NX, "z": NZ}

YL = 4
NB = NG // YL
Q = YL * NG
TERMS = 2
GROWS = 24
BCHUNK = 8
STEPS = NB // BCHUNK
CHUNK = BCHUNK * Q
F32 = jnp.float32
BF16 = jnp.bfloat16


def split_np(table):
    table = np.asarray(table, np.float32)
    high = table.astype(jnp.bfloat16)
    low = (table - high.astype(np.float32)).astype(jnp.bfloat16)
    return high, low


def tables():
    x = np.arange(NG)
    gx = np.arange(1, KX + 1)
    angle = 2 * math.pi / NG * ((gx[:, None] * x[None, :]) % NG)
    factor = np.zeros((GROWS, NG))
    for i in range(KX):
        factor[8 * (i // 4) + i % 4] = np.cos(angle[i])
        factor[8 * (i // 4) + 4 + i % 4] = -np.sin(angle[i])
    high, low = split_np(factor)
    x_table = np.concatenate([np.tile(high, (1, TERMS)), np.tile(low, (1, TERMS))], 0)
    b = np.arange(NB)
    gy = np.arange(KY)
    phi = 2 * math.pi / NB * ((gy[:, None] * b[None, :]) % NB)
    mix = np.zeros((2, 4, KY, NB, 8))
    for i in range(4):
        mix[0, i, :, :, i] = np.cos(phi)
        mix[0, i, :, :, 4 + i] = np.sin(phi)
        mix[1, i, :, :, 4 + i] = np.cos(phi)
        mix[1, i, :, :, i] = -np.sin(phi)
    mix = np.concatenate(split_np(mix.reshape(128, NB * 8)), 0)
    q = np.arange(Q)
    twist = 2 * math.pi / NG * (gy[:, None] * (q // NG)[None, :])
    twist = np.stack([np.cos(twist), np.sin(twist)]).astype(np.float32)
    gz = np.arange(KZ)
    theta = 2 * math.pi / NG * (((q % NG)[:, None] * gz[None, :]) % NG)
    cosine, sine = np.cos(theta), np.sin(theta)
    z_table = np.concatenate(
        [np.concatenate([cosine, -sine], 1), np.concatenate([sine, cosine], 1)], 0
    )
    z_table = np.concatenate(split_np(z_table), 1)
    return x_table, mix, twist, z_table


def split(value):
    high = value.astype(BF16)
    low = (value - high.astype(F32)).astype(BF16)
    return high, low


def dot(left, right):
    return jnp.dot(left, right, preferred_element_type=F32)


def lane_group(rows):
    return lax.broadcasted_iota(jnp.int32, (rows, LANES), 1) // 32


def quarters(sticks_2d, q, start, count, stride):
    total = None
    for k in range(CAP):
        part = sticks_2d[pl.ds(8 * start + k, count, stride=8 * stride), :]
        turn = (32 * (k - q)) % LANES
        moved = pltpu.roll(part, turn, 1) if turn else part
        total = moved if total is None else jnp.where(lane_group(count) == k, moved, total)
    return total


def pack(sticks_2d, out):
    for q in range(4):
        for s in range(5):
            value = quarters(sticks_2d, q, s, 32, 5)
            for y in range(4):
                start = 10 * (32 * y + q) + s
                out[pl.ds(start, 4, stride=40), :] = value[8 * y : 8 * y + 4]
                start = 10 * (32 * y + 16 + 4 * q) + s
                out[pl.ds(start, 4, stride=10), :] = value[8 * y + 4 : 8 * y + 8]
            for h in range(2):
                out[pl.ds(10 * (32 * q + 16 * h) + 5 + s, 16, stride=10), :] = quarters(
                    sticks_2d, q, 5 * h + s, 16, 10
                )


def transform_kernel(
    slot_v,
    slot_c,
    perm,
    energy_v,
    energy_c,
    v_ref,
    c_ref,
    x_table,
    mix,
    twist,
    z_table,
    out,
    zh,
    zl,
    natural,
    ordered,
    v_wide,
    c_wide,
):
    step = pl.program_id(0)
    v_wide[...] = v_ref[...].astype(F32)
    c_wide[...] = c_ref[...].astype(F32)
    for k in range(CAP):
        high, low = split(v_wide[slot_v[0, k]] * c_wide[slot_c[0, k]])
        x_part = dot(x_table[...], jnp.concatenate([high, low], 0))
        x_part = x_part[:GROWS] + x_part[GROWS:]
        for g in range(3):
            block = x_part[8 * g : 8 * g + 8]
            block = jnp.concatenate(
                [block[:, Q * i : Q * i + Q] for i in range(BCHUNK)], 0
            )
            row = pl.multiple_of(step * (8 * BCHUNK), 16)
            high, low = split(block)
            zh[g, pl.ds(row, 8 * BCHUNK), Q * k : Q * (k + 1)] = high
            zl[g, pl.ds(row, 8 * BCHUNK), Q * k : Q * (k + 1)] = low

    @pl.when(step == STEPS - 1)
    def _():
        turn_c = twist[0][None]
        turn_s = twist[1][None]
        for k in range(CAP):
            real, imag = [], []
            for g in range(3):
                mixed = dot(mix[...], zh[g, :, Q * k : Q * (k + 1)])
                mixed = mixed[:128] + mixed[128:]
                mixed += dot(mix[:128], zl[g, :, Q * k : Q * (k + 1)])
                count = 64 if g < 2 else 32
                real.append(mixed[:count])
                imag.append(mixed[64 : 64 + count])
            real = jnp.concatenate(real, 0).reshape(KX, KY, Q)
            imag = jnp.concatenate(imag, 0).reshape(KX, KY, Q)
            turned_real = (real * turn_c + imag * turn_s).reshape(NSTICK, Q)
            turned_imag = (imag * turn_c - real * turn_s).reshape(NSTICK, Q)
            high, low = split(jnp.concatenate([turned_real, turned_imag], 1))
            value = dot(high, z_table[...])
            value = value[:, :128] + value[:, 128:] + dot(low, z_table[:, :128])
            gap = energy_c[slot_c[0, k]] - energy_v[slot_v[0, k]]
            gap = jnp.full((1, LANES), gap, F32)
            value = value * (jnp.sqrt(1.0 / gap) * NG ** (-1.5))
            natural[pl.ds(k, NSTICK, stride=8), :] = value

        def move(s, carry):
            source = pl.multiple_of(8 * perm[s], 8)
            target = pl.multiple_of(8 * s, 8)
            ordered[pl.ds(target, 8), :] = natural[pl.ds(source, 8), :]
            return carry

        lax.fori_loop(0, NSTICK, move, 0, unroll=8)
        pack(ordered, out)


def transform(v, c, ev, ec, slot_v, slot_c, perm):
    consts = [jnp.asarray(t) for t in tables()]
    whole = lambda a: pl.BlockSpec(a.shape, lambda i, *_: (0,) * a.ndim)
    bands = pl.BlockSpec((2, NG, CHUNK), lambda i, *_: (0, 0, i))
    return pl.pallas_call(
        transform_kernel,
        name="transform",
        out_shape=jax.ShapeDtypeStruct((10 * DEVICES, LANES), F32),
        grid_spec=pltpu.PrefetchScalarGridSpec(
            num_scalar_prefetch=5,
            grid=(STEPS,),
            in_specs=[bands, bands] + [whole(t) for t in consts],
            out_specs=pl.BlockSpec((10 * DEVICES, LANES), lambda i, *_: (0, 0)),
            scratch_shapes=[
                pltpu.VMEM((3, NB * 8, CAP * Q), BF16),
                pltpu.VMEM((3, NB * 8, CAP * Q), BF16),
                pltpu.VMEM((8 * NSTICK, LANES), F32),
                pltpu.VMEM((8 * NSTICK, LANES), F32),
                pltpu.VMEM((2, NG, CHUNK), F32),
                pltpu.VMEM((2, NG, CHUNK), F32),
            ],
        ),
        cost_estimate=pl.CostEstimate(
            flops=4_000_000_000,
            bytes_accessed=9_000_000,
            transcendentals=0,
        ),
    )(slot_v, slot_c, perm, ev, ec, v, c, *consts)


def pieces_kernel(count_ref, x_ref, row_out, col_out):
    counts = jnp.broadcast_to(count_ref[...], (DEVICES, LANES))
    device = lax.broadcasted_iota(jnp.int32, (DEVICES, LANES), 0)
    lane = lax.broadcasted_iota(jnp.int32, (DEVICES, LANES), 1)
    offset = jnp.sum(jnp.where(lane < device, counts, 0), axis=1, keepdims=True)
    own = jnp.sum(jnp.where(lane == device, counts, 0), axis=1, keepdims=True)
    pair = lax.broadcasted_iota(jnp.int32, (DEVICES, PAIRS), 1)
    chosen = []
    for k in range(CAP):
        hit = jnp.logical_and(pair == offset + k, k < own)
        chosen.append(jnp.where(hit, 1.0, 0.0).astype(BF16))
    chosen = jnp.concatenate(chosen + chosen, 0)
    wide = []
    for s in range(10):
        turned = x_ref[pl.ds(s, DEVICES, stride=10), :].T
        wide.append(
            jnp.concatenate([turned[32 * k : 32 * k + 32] for k in range(CAP)], 1)
        )
    high, low = split(jnp.concatenate(wide, 0))
    total = dot(jnp.concatenate([high, low], 1), chosen)
    row_out[...] = total[:160]
    col_out[...] = total[160:]


def pieces(count, received):
    shape = jax.ShapeDtypeStruct((160, PAIRS), F32)
    return pl.pallas_call(
        pieces_kernel,
        name="pieces",
        compiler_params=pltpu.CompilerParams(vmem_limit_bytes=12 << 20),
        out_shape=(shape, shape),
        cost_estimate=pl.CostEstimate(
            flops=180_000_000, bytes_accessed=1_000_000, transcendentals=0
        ),
    )(count, received)


def columns_kernel(where, mine, theirs, out, flat):
    y, core = where[1], where[2]
    for other, source in enumerate((mine, theirs)):
        base = 640 * ((core + other) % 2)
        for m in range(4):
            there = (y + 4 - m) % 4
            for s in range(5):
                row = pl.multiple_of(base + 128 * s + 32 * there, 32)
                flat[pl.ds(row, 32), :] = source[m, 32 * s : 32 * s + 32, :]
    for i in range(10):
        high, low = split(-flat[128 * i : 128 * i + 128, :].T)
        out[0:256, 128 * i : 128 * i + 128] = high
        out[256:512, 128 * i : 128 * i + 128] = low
        out[512:768, 128 * i : 128 * i + 128] = high


def columns(where, mine, theirs):
    vmem = pl.BlockSpec(memory_space=pltpu.VMEM)
    return pl.pallas_call(
        columns_kernel,
        name="columns",
        compiler_params=pltpu.CompilerParams(vmem_limit_bytes=16 << 20),
        out_shape=jax.ShapeDtypeStruct((3 * PAIRS, 1280), BF16),
        in_specs=[pl.BlockSpec(memory_space=pltpu.SMEM), vmem, vmem],
        out_specs=vmem,
        scratch_shapes=[pltpu.VMEM((1280, PAIRS), F32)],
        cost_estimate=pl.CostEstimate(
            flops=2_000_000, bytes_accessed=3_000_000, transcendentals=0
        ),
    )(where, mine, theirs)


def product_kernel(count, where, *refs):
    gathered = refs[:count]
    b3, out, a3 = refs[count], refs[-2], refs[-1]
    step = pl.program_id(0)
    part = pl.program_id(1)
    for k in range(count):

        @pl.when(jnp.logical_and(step == k, part == 0))
        def _():
            for m in range(4):
                there = (where[3] + 4 - m) % 4
                for s in range(5):
                    row = pl.multiple_of(128 * s + 32 * there, 32)
                    high, low = split(gathered[k][m, 32 * s : 32 * s + 32, :])
                    a3[pl.ds(row, 32), 0:256] = high
                    a3[pl.ds(row, 32), 256:512] = high
                    a3[pl.ds(row, 32), 512:768] = low

    width = out.shape[1]
    lane = pl.multiple_of(width * part, width)
    for n in range(0, width, 256):
        out[:, n : n + 256] = dot(a3[...], b3[:, pl.ds(lane + n, 256)])


def response_blocks(where, order, gathered, b3, parts, held=None):
    vmem = pl.BlockSpec(memory_space=pltpu.VMEM)
    count = len(gathered)
    width = 1280 // parts

    def place(i, j, w):
        back = sum(jnp.where(i == n, order[n], 0) for n in range(count))
        return ((w[0] + 4 - back) % 4, j)

    extra = [] if held is None else [held]
    return pl.pallas_call(
        functools.partial(product_kernel, count),
        name="response",
        compiler_params=pltpu.CompilerParams(vmem_limit_bytes=24 << 20),
        out_shape=jax.ShapeDtypeStruct((2560, 1280), F32),
        grid_spec=pltpu.PrefetchScalarGridSpec(
            num_scalar_prefetch=1,
            grid=(count, parts),
            in_specs=[vmem] * (count + 1)
            + [pl.BlockSpec(memory_space=pl.ANY)] * len(extra),
            out_specs=pl.BlockSpec((640, width), place),
            scratch_shapes=[pltpu.VMEM((640, 768), BF16)],
        ),
        input_output_aliases={} if held is None else {count + 2: 0},
        cost_estimate=pl.CostEstimate(
            flops=count * 1_300_000_000,
            bytes_accessed=count * 4_000_000,
            transcendentals=0,
        ),
    )(where, *gathered, b3, *extra)


def shift(value, axis, k):
    n = AXIS[axis]
    return lax.ppermute(value, axis, [(i, (i + k) % n) for i in range(n)])


def gather(value, axis):
    got = [value]
    for k in range(1, AXIS[axis]):
        got.append(shift(value, axis, k))
    return got


def plane_gather(value, stage):
    got = [value]
    for k in range(1, 4):
        pairs = []
        for core in range(NCORE):
            for x in range(NX):
                for z in range(NZ):
                    if core == stage:
                        to = (x, (z + k) % NZ)
                    else:
                        to = ((x + k) % NX, z)
                    pairs.append(
                        (16 * core + 4 * x + z, 16 * core + 4 * to[0] + to[1])
                    )
        got.append(lax.ppermute(value, ("core", "x", "z"), pairs))
    return got


def exchange(value):
    value = value.reshape(DEVICES, 10, 1, LANES)
    value = lax.all_to_all(
        value, ("y", "core", "x", "z"), split_axis=0, concat_axis=0, tiled=True
    )
    return value.reshape(DEVICES * 10, LANES)


def compute(v, c, ev, ec, slot_v, slot_c, count, perm):
    packed = transform(v, c, ev, ec, slot_v, slot_c, perm)
    row, column = pieces(count.reshape(1, DEVICES), exchange(packed))
    x, y, core, z = (lax.axis_index(a) for a in ("x", "y", "core", "z"))
    where = jnp.stack([jnp.where(core == 0, x, z), y, core, jnp.where(core == 0, z, x)])
    where = where.astype(jnp.int32)
    row = jnp.stack(plane_gather(row, 0))
    row, column = lax.optimization_barrier((row, column))
    gathered = plane_gather(row, 1)
    mine = jnp.stack(gather(column, "y"))
    b3 = columns(where, mine, shift(mine, "core", 1))
    return response_blocks(where, (0, 1, 3, 2), [gathered[k] for k in (0, 1, 3, 2)], b3, 1)


def solution(mesh):
    fine = Mesh(mesh.devices.reshape(NY, NCORE, NX, NZ), ("y", "core", "x", "z"))
    every = ("y", "core", "x", "z")
    return jax.shard_map(
        compute,
        mesh=fine,
        in_specs=(
            P(every, None, None),
            P(every, None, None),
            P(every),
            P(every),
            P(every, None),
            P(every, None),
            P(),
            P(),
        ),
        out_specs=P(("y", "core"), ("x", "z")),
        check_vma=False,
    )
```

```python
import functools
import math

import jax
import jax.numpy as jnp
import numpy as np
from jax import lax
from jax.experimental import pallas as pl
from jax.experimental.pallas import tpu as pltpu
from jax.sharding import Mesh, PartitionSpec as P

NG = 96
KX = 10
KY = 16
KZ = 64
CAP = 4
NSTICK = 160
LANES = 128
NY, NCORE, NX, NZ = 4, 2, 4, 4
DEVICES = 128
PAIRS = 256
AXIS = {"y": NY, "core": NCORE, "x": NX, "z": NZ}

YL = 4
NB = NG // YL
Q = YL * NG
TERMS = 2
GROWS = 24
BCHUNK = 8
STEPS = NB // BCHUNK
CHUNK = BCHUNK * Q
F32 = jnp.float32
BF16 = jnp.bfloat16


def split_np(table):
    table = np.asarray(table, np.float32)
    high = table.astype(jnp.bfloat16)
    low = (table - high.astype(np.float32)).astype(jnp.bfloat16)
    return high, low


def tables():
    x = np.arange(NG)
    gx = np.arange(1, KX + 1)
    angle = 2 * math.pi / NG * ((gx[:, None] * x[None, :]) % NG)
    factor = np.zeros((GROWS, NG))
    for i in range(KX):
        factor[8 * (i // 4) + i % 4] = np.cos(angle[i])
        factor[8 * (i // 4) + 4 + i % 4] = -np.sin(angle[i])
    high, low = split_np(factor)
    x_table = np.concatenate([np.tile(high, (1, TERMS)), np.tile(low, (1, TERMS))], 0)
    b = np.arange(NB)
    gy = np.arange(KY)
    phi = 2 * math.pi / NB * ((gy[:, None] * b[None, :]) % NB)
    mix = np.zeros((2, 4, KY, NB, 8))
    for i in range(4):
        mix[0, i, :, :, i] = np.cos(phi)
        mix[0, i, :, :, 4 + i] = np.sin(phi)
        mix[1, i, :, :, 4 + i] = np.cos(phi)
        mix[1, i, :, :, i] = -np.sin(phi)
    mix = np.concatenate(split_np(mix.reshape(128, NB * 8)), 0)
    q = np.arange(Q)
    twist = 2 * math.pi / NG * (gy[:, None] * (q // NG)[None, :])
    twist = np.stack([np.cos(twist), np.sin(twist)]).astype(np.float32)
    gz = np.arange(KZ)
    theta = 2 * math.pi / NG * (((q % NG)[:, None] * gz[None, :]) % NG)
    cosine, sine = np.cos(theta), np.sin(theta)
    z_table = np.concatenate(
        [np.concatenate([cosine, -sine], 1), np.concatenate([sine, cosine], 1)], 0
    )
    z_table = np.concatenate(split_np(z_table), 1)
    return x_table, mix, twist, z_table


def split(value):
    high = value.astype(BF16)
    low = (value - high.astype(F32)).astype(BF16)
    return high, low


def dot(left, right):
    return jnp.dot(left, right, preferred_element_type=F32)


def lane_group(rows):
    return lax.broadcasted_iota(jnp.int32, (rows, LANES), 1) // 32


def quarters(sticks_2d, q, start, count, stride):
    total = None
    for k in range(CAP):
        part = sticks_2d[pl.ds(8 * start + k, count, stride=8 * stride), :]
        turn = (32 * (k - q)) % LANES
        moved = pltpu.roll(part, turn, 1) if turn else part
        total = moved if total is None else jnp.where(lane_group(count) == k, moved, total)
    return total


def pack(sticks_2d, out):
    for q in range(4):
        for s in range(5):
            value = quarters(sticks_2d, q, s, 32, 5)
            for y in range(4):
                start = 10 * (32 * y + q) + s
                out[pl.ds(start, 4, stride=40), :] = value[8 * y : 8 * y + 4]
                start = 10 * (32 * y + 16 + 4 * q) + s
                out[pl.ds(start, 4, stride=10), :] = value[8 * y + 4 : 8 * y + 8]
            for h in range(2):
                out[pl.ds(10 * (32 * q + 16 * h) + 5 + s, 16, stride=10), :] = quarters(
                    sticks_2d, q, 5 * h + s, 16, 10
                )


def transform_kernel(
    slot_v,
    slot_c,
    perm,
    energy_v,
    energy_c,
    v_ref,
    c_ref,
    x_table,
    mix,
    twist,
    z_table,
    out,
    zh,
    zl,
    natural,
    ordered,
    v_wide,
    c_wide,
):
    step = pl.program_id(0)
    v_wide[...] = v_ref[...].astype(F32)
    c_wide[...] = c_ref[...].astype(F32)
    for k in range(CAP):
        high, low = split(v_wide[slot_v[0, k]] * c_wide[slot_c[0, k]])
        x_part = dot(x_table[...], jnp.concatenate([high, low], 0))
        x_part = x_part[:GROWS] + x_part[GROWS:]
        for g in range(3):
            block = x_part[8 * g : 8 * g + 8]
            block = jnp.concatenate(
                [block[:, Q * i : Q * i + Q] for i in range(BCHUNK)], 0
            )
            row = pl.multiple_of(step * (8 * BCHUNK), 16)
            high, low = split(block)
            zh[g, pl.ds(row, 8 * BCHUNK), Q * k : Q * (k + 1)] = high
            zl[g, pl.ds(row, 8 * BCHUNK), Q * k : Q * (k + 1)] = low

    @pl.when(step == STEPS - 1)
    def _():
        turn_c = twist[0][None]
        turn_s = twist[1][None]
        for k in range(CAP):
            real, imag = [], []
            for g in range(3):
                mixed = dot(mix[...], zh[g, :, Q * k : Q * (k + 1)])
                mixed = mixed[:128] + mixed[128:]
                mixed += dot(mix[:128], zl[g, :, Q * k : Q * (k + 1)])
                count = 64 if g < 2 else 32
                real.append(mixed[:count])
                imag.append(mixed[64 : 64 + count])
            real = jnp.concatenate(real, 0).reshape(KX, KY, Q)
            imag = jnp.concatenate(imag, 0).reshape(KX, KY, Q)
            turned_real = (real * turn_c + imag * turn_s).reshape(NSTICK, Q)
            turned_imag = (imag * turn_c - real * turn_s).reshape(NSTICK, Q)
            high, low = split(jnp.concatenate([turned_real, turned_imag], 1))
            value = dot(high, z_table[...])
            value = value[:, :128] + value[:, 128:] + dot(low, z_table[:, :128])
            gap = energy_c[slot_c[0, k]] - energy_v[slot_v[0, k]]
            gap = jnp.full((1, LANES), gap, F32)
            value = value * (jnp.sqrt(1.0 / gap) * NG ** (-1.5))
            natural[pl.ds(k, NSTICK, stride=8), :] = value

        def move(s, carry):
            source = pl.multiple_of(8 * perm[s], 8)
            target = pl.multiple_of(8 * s, 8)
            ordered[pl.ds(target, 8), :] = natural[pl.ds(source, 8), :]
            return carry

        lax.fori_loop(0, NSTICK, move, 0, unroll=8)
        pack(ordered, out)


def transform(v, c, ev, ec, slot_v, slot_c, perm):
    consts = [jnp.asarray(t) for t in tables()]
    whole = lambda a: pl.BlockSpec(a.shape, lambda i, *_: (0,) * a.ndim)
    bands = pl.BlockSpec((2, NG, CHUNK), lambda i, *_: (0, 0, i))
    return pl.pallas_call(
        transform_kernel,
        name="transform",
        out_shape=jax.ShapeDtypeStruct((10 * DEVICES, LANES), F32),
        grid_spec=pltpu.PrefetchScalarGridSpec(
            num_scalar_prefetch=5,
            grid=(STEPS,),
            in_specs=[bands, bands] + [whole(t) for t in consts],
            out_specs=pl.BlockSpec((10 * DEVICES, LANES), lambda i, *_: (0, 0)),
            scratch_shapes=[
                pltpu.VMEM((3, NB * 8, CAP * Q), BF16),
                pltpu.VMEM((3, NB * 8, CAP * Q), BF16),
                pltpu.VMEM((8 * NSTICK, LANES), F32),
                pltpu.VMEM((8 * NSTICK, LANES), F32),
                pltpu.VMEM((2, NG, CHUNK), F32),
                pltpu.VMEM((2, NG, CHUNK), F32),
            ],
        ),
        cost_estimate=pl.CostEstimate(
            flops=4_000_000_000,
            bytes_accessed=9_000_000,
            transcendentals=0,
        ),
    )(slot_v, slot_c, perm, ev, ec, v, c, *consts)


def pieces_kernel(count_ref, x_ref, row_out, col_out):
    counts = jnp.broadcast_to(count_ref[...], (DEVICES, LANES))
    device = lax.broadcasted_iota(jnp.int32, (DEVICES, LANES), 0)
    lane = lax.broadcasted_iota(jnp.int32, (DEVICES, LANES), 1)
    offset = jnp.sum(jnp.where(lane < device, counts, 0), axis=1, keepdims=True)
    own = jnp.sum(jnp.where(lane == device, counts, 0), axis=1, keepdims=True)
    pair = lax.broadcasted_iota(jnp.int32, (DEVICES, PAIRS), 1)
    chosen = []
    for k in range(CAP):
        hit = jnp.logical_and(pair == offset + k, k < own)
        chosen.append(jnp.where(hit, 1.0, 0.0).astype(BF16))
    chosen = jnp.concatenate(chosen + chosen, 0)
    wide = []
    for s in range(10):
        turned = x_ref[pl.ds(s, DEVICES, stride=10), :].T
        wide.append(
            jnp.concatenate([turned[32 * k : 32 * k + 32] for k in range(CAP)], 1)
        )
    high, low = split(jnp.concatenate(wide, 0))
    total = dot(jnp.concatenate([high, low], 1), chosen)
    row_out[...] = total[:160]
    col_out[...] = total[160:]


def pieces(count, received):
    shape = jax.ShapeDtypeStruct((160, PAIRS), F32)
    return pl.pallas_call(
        pieces_kernel,
        name="pieces",
        compiler_params=pltpu.CompilerParams(vmem_limit_bytes=12 << 20),
        out_shape=(shape, shape),
        cost_estimate=pl.CostEstimate(
            flops=180_000_000, bytes_accessed=1_000_000, transcendentals=0
        ),
    )(count, received)


def columns_kernel(where, mine, theirs, out, flat):
    y, core = where[1], where[2]
    for other, source in enumerate((mine, theirs)):
        base = 640 * ((core + other) % 2)
        for m in range(4):
            there = (y + 4 - m) % 4
            for s in range(5):
                row = pl.multiple_of(base + 128 * s + 32 * there, 32)
                flat[pl.ds(row, 32), :] = source[m, 32 * s : 32 * s + 32, :]
    for i in range(10):
        high, low = split(-flat[128 * i : 128 * i + 128, :].T)
        out[0:256, 128 * i : 128 * i + 128] = high
        out[256:512, 128 * i : 128 * i + 128] = low
        out[512:768, 128 * i : 128 * i + 128] = high


def columns(where, mine, theirs):
    vmem = pl.BlockSpec(memory_space=pltpu.VMEM)
    return pl.pallas_call(
        columns_kernel,
        name="columns",
        compiler_params=pltpu.CompilerParams(vmem_limit_bytes=8 << 20),
        out_shape=jax.ShapeDtypeStruct((3 * PAIRS, 1280), BF16),
        in_specs=[pl.BlockSpec(memory_space=pltpu.SMEM), vmem, vmem],
        out_specs=vmem,
        scratch_shapes=[pltpu.VMEM((1280, PAIRS), F32)],
        cost_estimate=pl.CostEstimate(
            flops=2_000_000, bytes_accessed=3_000_000, transcendentals=0
        ),
    )(where, mine, theirs)


def product_kernel(count, where, *refs):
    gathered = refs[:count]
    b3, out, a3 = refs[count], refs[-2], refs[-1]
    step = pl.program_id(0)
    part = pl.program_id(1)
    for k in range(count):

        @pl.when(jnp.logical_and(step == k, part == 0))
        def _():
            for m in range(4):
                there = (where[3] + 4 - m) % 4
                for s in range(5):
                    row = pl.multiple_of(128 * s + 32 * there, 32)
                    high, low = split(gathered[k][m, 32 * s : 32 * s + 32, :])
                    a3[pl.ds(row, 32), 0:256] = high
                    a3[pl.ds(row, 32), 256:512] = high
                    a3[pl.ds(row, 32), 512:768] = low

    width = out.shape[1]
    lane = pl.multiple_of(width * part, width)
    for n in range(0, width, 256):
        out[:, n : n + 256] = dot(a3[...], b3[:, pl.ds(lane + n, 256)])


def response_blocks(where, order, gathered, b3, parts, held=None):
    vmem = pl.BlockSpec(memory_space=pltpu.VMEM)
    count = len(gathered)
    width = 1280 // parts

    def place(i, j, w):
        back = sum(jnp.where(i == n, order[n], 0) for n in range(count))
        return ((w[0] + 4 - back) % 4, j)

    extra = [] if held is None else [held]
    return pl.pallas_call(
        functools.partial(product_kernel, count),
        name="response",
        compiler_params=pltpu.CompilerParams(vmem_limit_bytes=16 << 20),
        out_shape=jax.ShapeDtypeStruct((2560, 1280), F32),
        grid_spec=pltpu.PrefetchScalarGridSpec(
            num_scalar_prefetch=1,
            grid=(count, parts),
            in_specs=[vmem] * (count + 1)
            + [pl.BlockSpec(memory_space=pl.ANY)] * len(extra),
            out_specs=pl.BlockSpec((640, width), place),
            scratch_shapes=[pltpu.VMEM((640, 768), BF16)],
        ),
        input_output_aliases={} if held is None else {count + 2: 0},
        cost_estimate=pl.CostEstimate(
            flops=count * 1_300_000_000,
            bytes_accessed=count * 4_000_000,
            transcendentals=0,
        ),
    )(where, *gathered, b3, *extra)


def shift(value, axis, k):
    n = AXIS[axis]
    return lax.ppermute(value, axis, [(i, (i + k) % n) for i in range(n)])


def gather(value, axis):
    got = [value]
    for k in range(1, AXIS[axis]):
        got.append(shift(value, axis, k))
    return got


def plane_gather(value, stage):
    got = [value]
    for k in range(1, 4):
        pairs = []
        for core in range(NCORE):
            for x in range(NX):
                for z in range(NZ):
                    if core == stage:
                        to = (x, (z + k) % NZ)
                    else:
                        to = ((x + k) % NX, z)
                    pairs.append(
                        (16 * core + 4 * x + z, 16 * core + 4 * to[0] + to[1])
                    )
        got.append(lax.ppermute(value, ("core", "x", "z"), pairs))
    return got


def exchange(value):
    value = value.reshape(DEVICES, 10, 1, LANES)
    value = lax.all_to_all(
        value, ("y", "core", "x", "z"), split_axis=0, concat_axis=0, tiled=True
    )
    return value.reshape(DEVICES * 10, LANES)


def compute(v, c, ev, ec, slot_v, slot_c, count, perm):
    packed = transform(v, c, ev, ec, slot_v, slot_c, perm)
    row, column = pieces(count.reshape(1, DEVICES), exchange(packed))
    x, y, core, z = (lax.axis_index(a) for a in ("x", "y", "core", "z"))
    where = jnp.stack([jnp.where(core == 0, x, z), y, core, jnp.where(core == 0, z, x)])
    where = where.astype(jnp.int32)
    row = jnp.stack(plane_gather(row, 0))
    gathered = plane_gather(row, 1)
    mine = jnp.stack(gather(column, "y"))
    b3 = columns(where, mine, shift(mine, "core", 1))
    out = response_blocks(where, (0,), gathered[:1], b3, 1)
    return response_blocks(where, (1, 3, 2), [gathered[k] for k in (1, 3, 2)], b3, 1, out)


def solution(mesh):
    fine = Mesh(mesh.devices.reshape(NY, NCORE, NX, NZ), ("y", "core", "x", "z"))
    every = ("y", "core", "x", "z")
    return jax.shard_map(
        compute,
        mesh=fine,
        in_specs=(
            P(every, None, None),
            P(every, None, None),
            P(every),
            P(every),
            P(every, None),
            P(every, None),
            P(),
            P(),
        ),
        out_specs=P(("y", "core"), ("x", "z")),
        check_vma=False,
    )
```

```python
import functools
import math

import jax
import jax.numpy as jnp
import numpy as np
from jax import lax
from jax.experimental import pallas as pl
from jax.experimental.pallas import tpu as pltpu
from jax.sharding import Mesh, PartitionSpec as P

NG = 96
KX = 10
KY = 16
KZ = 64
CAP = 4
NSTICK = 160
LANES = 128
NY, NCORE, NX, NZ = 4, 2, 4, 4
DEVICES = 128
PAIRS = 256
AXIS = {"y": NY, "core": NCORE, "x": NX, "z": NZ}

YL = 4
NB = NG // YL
Q = YL * NG
TERMS = 2
GROWS = 24
BCHUNK = 8
STEPS = NB // BCHUNK
CHUNK = BCHUNK * Q
F32 = jnp.float32
BF16 = jnp.bfloat16


def split_np(table):
    table = np.asarray(table, np.float32)
    high = table.astype(jnp.bfloat16)
    low = (table - high.astype(np.float32)).astype(jnp.bfloat16)
    return high, low


def tables():
    x = np.arange(NG)
    gx = np.arange(1, KX + 1)
    angle = 2 * math.pi / NG * ((gx[:, None] * x[None, :]) % NG)
    factor = np.zeros((GROWS, NG))
    for i in range(KX):
        factor[8 * (i // 4) + i % 4] = np.cos(angle[i])
        factor[8 * (i // 4) + 4 + i % 4] = -np.sin(angle[i])
    high, low = split_np(factor)
    x_table = np.concatenate([np.tile(high, (1, TERMS)), np.tile(low, (1, TERMS))], 0)
    b = np.arange(NB)
    gy = np.arange(KY)
    phi = 2 * math.pi / NB * ((gy[:, None] * b[None, :]) % NB)
    mix = np.zeros((2, 4, KY, NB, 8))
    for i in range(4):
        mix[0, i, :, :, i] = np.cos(phi)
        mix[0, i, :, :, 4 + i] = np.sin(phi)
        mix[1, i, :, :, 4 + i] = np.cos(phi)
        mix[1, i, :, :, i] = -np.sin(phi)
    mix = np.concatenate(split_np(mix.reshape(128, NB * 8)), 0)
    q = np.arange(Q)
    twist = 2 * math.pi / NG * (gy[:, None] * (q // NG)[None, :])
    twist = np.stack([np.cos(twist), np.sin(twist)]).astype(np.float32)
    gz = np.arange(KZ)
    theta = 2 * math.pi / NG * (((q % NG)[:, None] * gz[None, :]) % NG)
    cosine, sine = np.cos(theta), np.sin(theta)
    z_table = np.concatenate(
        [np.concatenate([cosine, -sine], 1), np.concatenate([sine, cosine], 1)], 0
    )
    z_table = np.concatenate(split_np(z_table), 1)
    return x_table, mix, twist, z_table


def split(value):
    high = value.astype(BF16)
    low = (value - high.astype(F32)).astype(BF16)
    return high, low


def dot(left, right):
    return jnp.dot(left, right, preferred_element_type=F32)


def lane_group(rows):
    return lax.broadcasted_iota(jnp.int32, (rows, LANES), 1) // 32


def quarters(sticks_2d, q, start, count, stride):
    total = None
    for k in range(CAP):
        part = sticks_2d[pl.ds(8 * start + k, count, stride=8 * stride), :]
        turn = (32 * (k - q)) % LANES
        moved = pltpu.roll(part, turn, 1) if turn else part
        total = moved if total is None else jnp.where(lane_group(count) == k, moved, total)
    return total


def pack(sticks_2d, out):
    for q in range(4):
        for s in range(5):
            value = quarters(sticks_2d, q, s, 32, 5)
            for y in range(4):
                start = 10 * (32 * y + q) + s
                out[pl.ds(start, 4, stride=40), :] = value[8 * y : 8 * y + 4]
                start = 10 * (32 * y + 16 + 4 * q) + s
                out[pl.ds(start, 4, stride=10), :] = value[8 * y + 4 : 8 * y + 8]
            for h in range(2):
                out[pl.ds(10 * (32 * q + 16 * h) + 5 + s, 16, stride=10), :] = quarters(
                    sticks_2d, q, 5 * h + s, 16, 10
                )


def transform_kernel(
    slot_v,
    slot_c,
    perm,
    energy_v,
    energy_c,
    v_ref,
    c_ref,
    x_table,
    mix,
    twist,
    z_table,
    out,
    zh,
    zl,
    natural,
    ordered,
):
    step = pl.program_id(0)
    for k in range(CAP):
        left = v_ref[slot_v[0, k]].astype(F32)
        right = c_ref[slot_c[0, k]].astype(F32)
        high, low = split(left * right)
        x_part = dot(x_table[...], jnp.concatenate([high, low], 0))
        x_part = x_part[:GROWS] + x_part[GROWS:]
        for g in range(3):
            block = x_part[8 * g : 8 * g + 8]
            block = jnp.concatenate(
                [block[:, Q * i : Q * i + Q] for i in range(BCHUNK)], 0
            )
            row = pl.multiple_of(step * (8 * BCHUNK), 16)
            high, low = split(block)
            zh[g, pl.ds(row, 8 * BCHUNK), Q * k : Q * (k + 1)] = high
            zl[g, pl.ds(row, 8 * BCHUNK), Q * k : Q * (k + 1)] = low

    @pl.when(step == STEPS - 1)
    def _():
        turn_c = twist[0][None]
        turn_s = twist[1][None]
        for k in range(CAP):
            real, imag = [], []
            for g in range(3):
                mixed = dot(mix[...], zh[g, :, Q * k : Q * (k + 1)])
                mixed = mixed[:128] + mixed[128:]
                mixed += dot(mix[:128], zl[g, :, Q * k : Q * (k + 1)])
                count = 64 if g < 2 else 32
                real.append(mixed[:count])
                imag.append(mixed[64 : 64 + count])
            real = jnp.concatenate(real, 0).reshape(KX, KY, Q)
            imag = jnp.concatenate(imag, 0).reshape(KX, KY, Q)
            turned_real = (real * turn_c + imag * turn_s).reshape(NSTICK, Q)
            turned_imag = (imag * turn_c - real * turn_s).reshape(NSTICK, Q)
            high, low = split(jnp.concatenate([turned_real, turned_imag], 1))
            value = dot(high, z_table[...])
            value = value[:, :128] + value[:, 128:] + dot(low, z_table[:, :128])
            gap = energy_c[slot_c[0, k]] - energy_v[slot_v[0, k]]
            gap = jnp.full((1, LANES), gap, F32)
            value = value * (jnp.sqrt(1.0 / gap) * NG ** (-1.5))
            natural[pl.ds(k, NSTICK, stride=8), :] = value

        def move(s, carry):
            source = pl.multiple_of(8 * perm[s], 8)
            target = pl.multiple_of(8 * s, 8)
            ordered[pl.ds(target, 8), :] = natural[pl.ds(source, 8), :]
            return carry

        lax.fori_loop(0, NSTICK, move, 0, unroll=8)
        pack(ordered, out)


def transform(v, c, ev, ec, slot_v, slot_c, perm):
    consts = [jnp.asarray(t) for t in tables()]
    whole = lambda a: pl.BlockSpec(a.shape, lambda i, *_: (0,) * a.ndim)
    bands = pl.BlockSpec((2, NG, CHUNK), lambda i, *_: (0, 0, i))
    return pl.pallas_call(
        transform_kernel,
        name="transform",
        out_shape=jax.ShapeDtypeStruct((10 * DEVICES, LANES), F32),
        grid_spec=pltpu.PrefetchScalarGridSpec(
            num_scalar_prefetch=5,
            grid=(STEPS,),
            in_specs=[bands, bands] + [whole(t) for t in consts],
            out_specs=pl.BlockSpec((10 * DEVICES, LANES), lambda i, *_: (0, 0)),
            scratch_shapes=[
                pltpu.VMEM((3, NB * 8, CAP * Q), BF16),
                pltpu.VMEM((3, NB * 8, CAP * Q), BF16),
                pltpu.VMEM((8 * NSTICK, LANES), F32),
                pltpu.VMEM((8 * NSTICK, LANES), F32),
            ],
        ),
        cost_estimate=pl.CostEstimate(
            flops=4_000_000_000,
            bytes_accessed=9_000_000,
            transcendentals=0,
        ),
    )(slot_v, slot_c, perm, ev, ec, v, c, *consts)


def pieces_kernel(count_ref, x_ref, row_out, col_out):
    counts = jnp.broadcast_to(count_ref[...], (DEVICES, LANES))
    device = lax.broadcasted_iota(jnp.int32, (DEVICES, LANES), 0)
    lane = lax.broadcasted_iota(jnp.int32, (DEVICES, LANES), 1)
    offset = jnp.sum(jnp.where(lane < device, counts, 0), axis=1, keepdims=True)
    own = jnp.sum(jnp.where(lane == device, counts, 0), axis=1, keepdims=True)
    pair = lax.broadcasted_iota(jnp.int32, (DEVICES, PAIRS), 1)
    chosen = []
    for k in range(CAP):
        hit = jnp.logical_and(pair == offset + k, k < own)
        chosen.append(jnp.where(hit, 1.0, 0.0).astype(BF16))
    chosen = jnp.concatenate(chosen + chosen, 0)
    wide = []
    for s in range(10):
        turned = x_ref[pl.ds(s, DEVICES, stride=10), :].T
        wide.append(
            jnp.concatenate([turned[32 * k : 32 * k + 32] for k in range(CAP)], 1)
        )
    high, low = split(jnp.concatenate(wide, 0))
    total = dot(jnp.concatenate([high, low], 1), chosen)
    row_out[...] = total[:160]
    col_out[...] = total[160:]


def pieces(count, received):
    shape = jax.ShapeDtypeStruct((160, PAIRS), F32)
    return pl.pallas_call(
        pieces_kernel,
        name="pieces",
        compiler_params=pltpu.CompilerParams(vmem_limit_bytes=12 << 20),
        out_shape=(shape, shape),
        cost_estimate=pl.CostEstimate(
            flops=180_000_000, bytes_accessed=1_000_000, transcendentals=0
        ),
    )(count, received)


def columns_kernel(where, mine, theirs, out, flat):
    y, core = where[1], where[2]
    for other, source in enumerate((mine, theirs)):
        base = 640 * ((core + other) % 2)
        for m in range(4):
            there = (y + 4 - m) % 4
            for s in range(5):
                row = pl.multiple_of(base + 128 * s + 32 * there, 32)
                flat[pl.ds(row, 32), :] = source[m, 32 * s : 32 * s + 32, :]
    for i in range(10):
        high, low = split(-flat[128 * i : 128 * i + 128, :].T)
        out[0:256, 128 * i : 128 * i + 128] = high
        out[256:512, 128 * i : 128 * i + 128] = low
        out[512:768, 128 * i : 128 * i + 128] = high


def columns(where, mine, theirs):
    vmem = pl.BlockSpec(memory_space=pltpu.VMEM)
    return pl.pallas_call(
        columns_kernel,
        name="columns",
        compiler_params=pltpu.CompilerParams(vmem_limit_bytes=8 << 20),
        out_shape=jax.ShapeDtypeStruct((3 * PAIRS, 1280), BF16),
        in_specs=[pl.BlockSpec(memory_space=pltpu.SMEM), vmem, vmem],
        out_specs=vmem,
        scratch_shapes=[pltpu.VMEM((1280, PAIRS), F32)],
        cost_estimate=pl.CostEstimate(
            flops=2_000_000, bytes_accessed=3_000_000, transcendentals=0
        ),
    )(where, mine, theirs)


def product_kernel(count, where, *refs):
    gathered = refs[:count]
    b3, out, a3 = refs[count], refs[-2], refs[-1]
    step = pl.program_id(0)
    part = pl.program_id(1)
    for k in range(count):

        @pl.when(jnp.logical_and(step == k, part == 0))
        def _():
            for m in range(4):
                there = (where[3] + 4 - m) % 4
                for s in range(5):
                    row = pl.multiple_of(128 * s + 32 * there, 32)
                    high, low = split(gathered[k][m, 32 * s : 32 * s + 32, :])
                    a3[pl.ds(row, 32), 0:256] = high
                    a3[pl.ds(row, 32), 256:512] = high
                    a3[pl.ds(row, 32), 512:768] = low

    width = out.shape[1]
    lane = pl.multiple_of(width * part, width)
    for n in range(0, width, 256):
        out[:, n : n + 256] = dot(a3[...], b3[:, pl.ds(lane + n, 256)])


def response_blocks(where, order, gathered, b3, parts, held=None):
    vmem = pl.BlockSpec(memory_space=pltpu.VMEM)
    count = len(gathered)
    width = 1280 // parts

    def place(i, j, w):
        back = sum(jnp.where(i == n, order[n], 0) for n in range(count))
        return ((w[0] + 4 - back) % 4, j)

    extra = [] if held is None else [held]
    return pl.pallas_call(
        functools.partial(product_kernel, count),
        name="response",
        compiler_params=pltpu.CompilerParams(vmem_limit_bytes=16 << 20),
        out_shape=jax.ShapeDtypeStruct((2560, 1280), F32),
        grid_spec=pltpu.PrefetchScalarGridSpec(
            num_scalar_prefetch=1,
            grid=(count, parts),
            in_specs=[vmem] * (count + 1)
            + [pl.BlockSpec(memory_space=pl.ANY)] * len(extra),
            out_specs=pl.BlockSpec((640, width), place),
            scratch_shapes=[pltpu.VMEM((640, 768), BF16)],
        ),
        input_output_aliases={} if held is None else {count + 2: 0},
        cost_estimate=pl.CostEstimate(
            flops=count * 1_300_000_000,
            bytes_accessed=count * 4_000_000,
            transcendentals=0,
        ),
    )(where, *gathered, b3, *extra)


def shift(value, axis, k):
    n = AXIS[axis]
    return lax.ppermute(value, axis, [(i, (i + k) % n) for i in range(n)])


def gather(value, axis):
    got = [value]
    for k in range(1, AXIS[axis]):
        got.append(shift(value, axis, k))
    return got


def plane_gather(value, stage):
    got = [value]
    for k in range(1, 4):
        pairs = []
        for core in range(NCORE):
            for x in range(NX):
                for z in range(NZ):
                    if core == stage:
                        to = (x, (z + k) % NZ)
                    else:
                        to = ((x + k) % NX, z)
                    pairs.append(
                        (16 * core + 4 * x + z, 16 * core + 4 * to[0] + to[1])
                    )
        got.append(lax.ppermute(value, ("core", "x", "z"), pairs))
    return got


def exchange(value):
    value = value.reshape(DEVICES, 10, 1, LANES)
    value = lax.all_to_all(
        value, ("y", "core", "x", "z"), split_axis=0, concat_axis=0, tiled=True
    )
    return value.reshape(DEVICES * 10, LANES)


def compute(v, c, ev, ec, slot_v, slot_c, count, perm):
    packed = transform(v, c, ev, ec, slot_v, slot_c, perm)
    row, column = pieces(count.reshape(1, DEVICES), exchange(packed))
    x, y, core, z = (lax.axis_index(a) for a in ("x", "y", "core", "z"))
    where = jnp.stack([jnp.where(core == 0, x, z), y, core, jnp.where(core == 0, z, x)])
    where = where.astype(jnp.int32)
    row = jnp.stack(plane_gather(row, 0))
    gathered = plane_gather(row, 1)
    mine = jnp.stack(gather(column, "y"))
    b3 = columns(where, mine, shift(mine, "core", 1))
    out = response_blocks(where, (0,), gathered[:1], b3, 1)
    return response_blocks(where, (1, 3, 2), [gathered[k] for k in (1, 3, 2)], b3, 1, out)


def solution(mesh):
    fine = Mesh(mesh.devices.reshape(NY, NCORE, NX, NZ), ("y", "core", "x", "z"))
    every = ("y", "core", "x", "z")
    return jax.shard_map(
        compute,
        mesh=fine,
        in_specs=(
            P(every, None, None),
            P(every, None, None),
            P(every),
            P(every),
            P(every, None),
            P(every, None),
            P(),
            P(),
        ),
        out_specs=P(("y", "core"), ("x", "z")),
        check_vma=False,
    )
```
